32 devices in a mesh: dp: 8 (over y, x, core), tensor: 4 (over z).
Axes of the slice: x: 2, y: 2, z: 4, core: 2. Of those that a mesh axis runs over, the one named last changes fastest.
Arguments:
- tokens: bfloat16 [32768, 768], P(('dp', 'tensor')), may hold values from -6 to 6
- segments: int32 [64, 512], P(('dp', 'tensor')), may hold values from 0 to 3, never falling along the last dimension, each value on 1 to 256 neighbouring positions
- qkv_weight: bfloat16 [768, 2304], replicated, may hold values from -0.21875 to 0.21875
- qv_bias: bfloat16 [1536], replicated, may hold values from -3 to 3
- out_weight: bfloat16 [768, 768], replicated, may hold values from -1.25 to 1.25
- out_bias: bfloat16 [768], replicated, may hold values from -3 to 3
- gain_one: bfloat16 [768], replicated, may hold values from 0.5 to 1.5
- shift_one: bfloat16 [768], replicated, may hold values from -2 to 2
- up_weight: bfloat16 [768, 3072], P(None, 'tensor'), may hold values from -0.21875 to 0.21875
- up_bias: bfloat16 [3072], P('tensor'), may hold values from -3 to 3
- down_weight: bfloat16 [3072, 768], P('tensor'), may hold values from -0.109375 to 0.109375
- down_bias: bfloat16 [768], replicated, may hold values from -2 to 2
- gain_two: bfloat16 [768], replicated, may hold values from 0.5 to 1.5
- shift_two: bfloat16 [768], replicated, may hold values from -2 to 2
- mask_logits: bfloat16 [12, 512, 512], replicated, may hold values from -6 to 6
- mask_noise: bfloat16 [12, 512, 512], replicated, may hold values from -5 to 5
- cotangent: bfloat16 [32768, 768], P(('dp', 'tensor')), may hold values from -6 to 6
Outputs:
- output: bfloat16 [32768, 768], P(('dp', 'tensor'))
- tokens_grad: float32 [32768, 768], P(('dp', 'tensor'))
- qkv_weight_grad: float32 [768, 2304], replicated
- qv_bias_grad: float32 [1536], replicated
- out_weight_grad: float32 [768, 768], replicated
- out_bias_grad: float32 [768], replicated
- gain_one_grad: float32 [768], replicated
- shift_one_grad: float32 [768], replicated
- up_weight_grad: float32 [768, 3072], P(None, 'tensor')
- up_bias_grad: float32 [3072], P('tensor')
- down_weight_grad: float32 [3072, 768], P('tensor')
- down_bias_grad: float32 [768], replicated
- gain_two_grad: float32 [768], replicated
- shift_two_grad: float32 [768], replicated
- mask_logits_grad: float32 [12, 512, 512], P(None, 'dp', 'tensor')
The draws below stay inside these ranges and needn't reach their ends.
Inputs may be any that keep to these rules, and one draw needn't show every extreme that they name: `segments`: along each row the numbers never fall; equal numbers mark one packed document of at most 256 positions.
All inputs are finite; a program needn't handle non-finite values.
Results may differ from the reference program's by a relative error of at most 0.014.
Values may be sent and summed in bfloat16 or wider, within the bound.
No kernel may reach another device: no remote copies, remote signals or barrier semaphores. Data moves between devices by JAX's collectives and lax.ppermute only.
A program may use at most 192 MiB of HBM per device.

```python
import math
import jax
import jax.numpy as jnp
import numpy as np
from jax import lax

D = 768
H = 12
HD = 64
FF = 3072
S = 512
ROWS = 64
TOKENS = 32768


def steps_of(rng, dims, shards, least, top_value):
    def one(axis_at, parts):
        steps = jax.random.uniform(jax.random.fold_in(jax.random.fold_in(rng, 6), axis_at), (parts,), jnp.float32, least / len(shards), top_value / len(shards))
        return jnp.repeat(jnp.exp(steps), dims[axis_at] // parts).reshape((-1,) + (1,) * (len(dims) - axis_at - 1))

    loudness = one(*shards[0])
    for cut in shards[1:]:
        loudness = loudness * one(*cut)
    return loudness


def profile(count, total, bound, skew):
    loads = [(1 << 20) // math.isqrt(grade ** skew) + 1 for grade in range(2, count + 1)]
    surplus, counts = total - bound - (count - 1), [1] * (count - 1)
    while surplus > 0:
        free = [i for i in range(count - 1) if counts[i] < bound]
        pool, budget = sum([loads[i] for i in free]), surplus
        for i in free:
            more = min(bound - counts[i], max(1, budget * loads[i] // pool), surplus)
            counts[i] = counts[i] + more
            surplus = surplus - more
    return np.array([bound] + counts)


def uneven(key, number_of, total, limit, lean):
    if number_of == 2:
        one = jax.random.randint(key, (), max(1, total - limit), min(limit, total - 1) + 1)
        return jnp.stack([one, total - one])
    tallies = jnp.asarray(profile(number_of, total, limit, lean), jnp.int32)
    twos = (number_of - 1) // 2
    source_of, receiver = tallies[1:1 + 2 * twos:2], tallies[2:2 + 2 * twos:2]
    room = jnp.minimum(source_of - 1, limit - receiver)
    moved = jax.random.randint(jax.random.fold_in(key, 1), (twos,), 0, 1 << 20) % (room + 1)
    tallies = tallies.at[1:1 + 2 * twos:2].set(source_of - moved).at[2:2 + 2 * twos:2].set(receiver + moved)
    return tallies[jax.random.permutation(jax.random.fold_in(key, 2), number_of)]


def gaussian(rng, dims, scale, most, shards=(), held_as=jnp.bfloat16):
    values = jax.random.normal(rng, dims, jnp.float32) * scale
    if len(shards) > 0:
        values = steps_of(rng, dims, shards, -0.22, 0.18) * values
    return jnp.clip(values, min=-most, max=most).astype(held_as)


def setup_inputs(seed: int = 0) -> dict:
    key_list = jax.random.split(jax.random.key(seed), 18)
    tokens = gaussian(key_list[0], (TOKENS, D), 1.0, 6.0, ((0, 32),))
    segments = jax.vmap(lambda own: jnp.searchsorted(jnp.cumsum(uneven(own, max(4, S // 128), S, S // 2, 2)), jnp.arange(S), side="right"))(jax.random.split(key_list[1], ROWS)).reshape((ROWS, S)).astype(jnp.int32)
    qkv_weight = gaussian(key_list[2], (D, 3 * D), D ** -0.5, 0.21875)
    qv_bias = gaussian(key_list[3], (2 * D,), 0.5, 3.0)
    out_weight = gaussian(key_list[4], (D, D), (D // 32) ** -0.5, 1.25)
    out_bias = gaussian(key_list[5], (D,), 0.5, 3.0)
    gain_one = jnp.clip(1.0 + 0.1 * jax.random.normal(key_list[6], (D,), jnp.float32), 0.5, 1.5).astype(jnp.bfloat16)
    shift_one = gaussian(key_list[7], (D,), 0.3, 2.0)
    up_weight = gaussian(key_list[8], (D, FF), D ** -0.5, 0.21875, ((1, 4),))
    up_bias = gaussian(key_list[9], (FF,), 0.5, 3.0, ((0, 4),))
    down_weight = gaussian(key_list[10], (FF, D), FF ** -0.5, 0.109375, ((0, 4),))
    down_bias = gaussian(key_list[11], (D,), 0.3, 2.0)
    gain_two = jnp.clip(1.0 + 0.1 * jax.random.normal(key_list[12], (D,), jnp.float32), 0.5, 1.5).astype(jnp.bfloat16)
    shift_two = gaussian(key_list[13], (D,), 0.3, 2.0)
    mask_logits = gaussian(key_list[14], (H, S, S), 1.5, 6.0)
    mask_noise = gaussian(key_list[15], (H, S, S), 1.0, 5.0)
    cotangent = gaussian(key_list[16], (TOKENS, D), 1.0, 6.0, ((0, 32),))
    return {"tokens": tokens, "segments": segments, "qkv_weight": qkv_weight, "qv_bias": qv_bias, "out_weight": out_weight, "out_bias": out_bias, "gain_one": gain_one, "shift_one": shift_one, "up_weight": up_weight, "up_bias": up_bias, "down_weight": down_weight, "down_bias": down_bias, "gain_two": gain_two, "shift_two": shift_two, "mask_logits": mask_logits, "mask_noise": mask_noise, "cotangent": cotangent}


@jax.custom_vjp
def low(v):
    return lax.optimization_barrier(v.astype(jnp.bfloat16)).astype(jnp.float32)

@jax.custom_vjp
def low_back(v):
    return v

def low_keep(v):
    return (low(v), None)

def low_pass(kept, grad):
    return (grad,)

def back_keep(v):
    return (v, None)

def back_low(kept, grad):
    return (low(grad),)
low.defvjp(low_keep, low_pass)
low_back.defvjp(back_keep, back_low)
epsilon = 1e-12
negative = -1e+30

def layer_norm(values, gain_vec, shift_vec):
    average = lax.optimization_barrier(jnp.mean(values, axis=-1, keepdims=True))
    centred = values - average
    variance = lax.optimization_barrier(jnp.mean(centred * centred, axis=-1, keepdims=True))
    return centred * lax.rsqrt(variance + epsilon) * gain_vec + shift_vec

def gelu_exact(values):
    return jax.nn.gelu(values, approximate=False)

def forward(tokens, qkv_weight, qv_bias, out_weight, out_bias, gain_one, shift_one, up_weight, up_bias, down_weight, down_bias, gain_two, shift_two, mask_logits, mask_noise, segments):
    highest = lax.Precision.HIGHEST
    key_zeros = jnp.zeros((D,), jnp.float32)
    full_bias = jnp.concatenate([qv_bias[:D], key_zeros, qv_bias[D:]])
    projected = low_back(low(jnp.dot(tokens, qkv_weight, precision=highest) + full_bias))
    head_blocks = projected.reshape(segments.shape[0], S, 3, H, HD)
    mask_term = jax.nn.log_sigmoid(mask_logits + mask_noise)

    def one_row(row_pair):
        row_block, segment_row = row_pair
        scores = jnp.einsum('qhd,khd->hqk', row_block[:, 0], row_block[:, 1], precision=highest) * HD ** (-0.5) + mask_term
        same_doc = segment_row[:, None] == segment_row[None, :]
        scores = low_back(jnp.where(same_doc[None], scores, negative))
        weights = low(jax.nn.softmax(scores, axis=-1))
        return jnp.einsum('hqk,khd->qhd', weights, row_block[:, 2], precision=highest)
    attended = lax.map(jax.checkpoint(one_row), (head_blocks, segments))
    attended = low_back(low(attended.reshape(tokens.shape[0], D)))
    branch = low_back(jnp.dot(attended, out_weight, precision=highest) + out_bias)
    first_norm = layer_norm(tokens + branch, gain_one, shift_one)
    hidden_pre = low_back(jnp.dot(low(first_norm), up_weight, precision=highest) + up_bias)
    hidden = low(gelu_exact(hidden_pre))
    feed_out = low_back(jnp.dot(hidden, down_weight, precision=highest) + down_bias)
    return layer_norm(first_norm + feed_out, gain_two, shift_two)

def reference(tokens, segments, qkv_weight, qv_bias, out_weight, out_bias, gain_one, shift_one, up_weight, up_bias, down_weight, down_bias, gain_two, shift_two, mask_logits, mask_noise, cotangent):
    noise_float = mask_noise.astype(jnp.float32)
    inputs = tuple((array.astype(jnp.float32) for array in (tokens, qkv_weight, qv_bias, out_weight, out_bias, gain_one, shift_one, up_weight, up_bias, down_weight, down_bias, gain_two, shift_two, mask_logits)))
    output, backward = jax.vjp(lambda *params: forward(*params, noise_float, segments), *inputs)
    gradients = backward(cotangent.astype(jnp.float32))
    return (output.astype(jnp.bfloat16), gradients[0], gradients[1], gradients[2], gradients[3], gradients[4], gradients[5], gradients[6], gradients[7], gradients[8], gradients[9], gradients[10], gradients[11], gradients[12], gradients[13])
```

```python
import jax
import jax.numpy as jnp
from jax import lax
from jax.sharding import PartitionSpec as P

D = 768
H = 12
HD = 64
S = 512
AXES = ("dp", "tensor")
BF = jnp.bfloat16
F32 = jnp.float32

epsilon = 1e-12
negative = -1e30


def layer_norm(values, gain_vec, shift_vec):
    average = jnp.mean(values, axis=-1, keepdims=True)
    centred = values - average
    variance = jnp.mean(centred * centred, axis=-1, keepdims=True)
    return centred * lax.rsqrt(variance + epsilon) * gain_vec + shift_vec


def gelu_exact(values):
    return jax.nn.gelu(values, approximate=False)


def row_scores(row_block, segment_row, mask_term):
    heads_view = row_block.reshape(S, 3, H, HD)
    scores = jnp.einsum(
        "qhd,khd->hqk", heads_view[:, 0], heads_view[:, 1], preferred_element_type=jnp.float32
    )
    scores = scores * HD ** (-0.5) + mask_term
    same_doc = segment_row[:, None] == segment_row[None, :]
    return (jnp.where(same_doc[None], scores, negative), heads_view)


class Exchange:
    def __init__(self, n_dp, n_tensor):
        self.count = n_dp * n_tensor
        self.tensor_bits = list(range(n_tensor.bit_length() - 1))
        first = len(self.tensor_bits)
        self.dp_bits = list(range(first, first + n_dp.bit_length() - 1))
        self.index = lax.axis_index("dp") * n_tensor + lax.axis_index("tensor")

    def orders(self):
        near, rest = self.dp_bits[0], self.dp_bits[1:]
        low, high = self.tensor_bits[:1], self.tensor_bits[1:]
        return (
            [near] + rest + low + high,
            [near] + rest[1:] + low + rest[:1] + high,
            [near] + low + rest + high,
        )

    def bit(self, b):
        return (self.index >> b) & 1

    def swap(self, x, b):
        return lax.ppermute(x, AXES, [(i, i ^ (1 << b)) for i in range(self.count)])

    def reduce(self, x, axes, order):
        axes = list(axes)
        for b in order:
            at = axes.index(b)
            mine = self.bit(b)
            sent = lax.dynamic_index_in_dim(x, 1 - mine, at, keepdims=False).astype(BF)
            kept = lax.dynamic_index_in_dim(x, mine, at, keepdims=False)
            got = self.swap(sent, b)
            x = (kept.astype(F32) + got.astype(F32)).astype(BF)
            axes.pop(at)
        return x

    def gather(self, x, order):
        for b in order:
            got = self.swap(x, b)
            mine = self.bit(b) == 1
            x = jnp.stack([jnp.where(mine, got, x), jnp.where(mine, x, got)])
        return x

    def total(self, x, order):
        for b in order:
            x = x + self.swap(x, b)
        return x


def to_order(x, have, want):
    n = len(have)
    return jnp.transpose(x, [have.index(b) for b in want] + list(range(n, x.ndim)))


def local(
    tokens,
    segments,
    qkv_weight,
    qv_bias,
    out_weight,
    out_bias,
    gain_one,
    shift_one,
    up_weight,
    up_bias,
    down_weight,
    down_bias,
    gain_two,
    shift_two,
    mask_logits,
    mask_noise,
    cotangent,
    *,
    n_dp,
    n_tensor,
):
    ex = Exchange(n_dp, n_tensor)
    orders = ex.orders()
    tb, db = ex.tensor_bits[::-1], ex.dp_bits[::-1]
    tw, dw = [2] * len(tb), [2] * len(db)
    local_rows = tokens.shape[0]
    row_count = segments.shape[0]
    fs = up_weight.shape[1]
    dp_at = lax.axis_index("dp")

    third = D // 3
    part = third // n_dp
    gathered = []
    for g, order in enumerate(orders):
        mine = jnp.stack(
            [
                lax.dynamic_slice_in_dim(up_weight, g * third + dp_at * part, part, 0),
                lax.dynamic_slice_in_dim(down_weight, g * third + dp_at * part, part, 0),
            ]
        )
        full = ex.gather(mine, order[::-1])
        full = to_order(full, order, tb + db)
        full = full.reshape((n_tensor, n_dp, 2, part, D))
        gathered.append(full.transpose(2, 0, 1, 3, 4).reshape(2, n_tensor, third, D))
    weights_all = jnp.concatenate(gathered, axis=2)
    up_all, down_all = weights_all[0], weights_all[1]
    up_bias_all = ex.gather(up_bias, ex.tensor_bits).reshape(n_tensor, fs)

    qv_float = qv_bias.astype(jnp.float32)
    full_bias = jnp.concatenate([qv_float[:D], jnp.zeros((D,), jnp.float32), qv_float[D:]])
    projected = jnp.dot(tokens, qkv_weight, preferred_element_type=jnp.float32) + full_bias
    qkv_rows = projected.astype(jnp.bfloat16).reshape(row_count, S, 3 * D)
    mask_sum = mask_logits.astype(jnp.float32) + mask_noise.astype(jnp.float32)
    mask_term = jax.nn.log_sigmoid(mask_sum)

    def attend(row_pair):
        row_block, segment_row = row_pair
        scores, heads_view = row_scores(row_block, segment_row, mask_term)
        peak_score = jnp.max(scores, axis=-1, keepdims=True)
        expo_vals = jnp.exp(scores - peak_score)
        sum_total = jnp.sum(expo_vals, axis=-1, keepdims=True)
        weights = (expo_vals / sum_total).astype(jnp.bfloat16)
        context = jnp.einsum(
            "hqk,khd->qhd", weights, heads_view[:, 2], preferred_element_type=jnp.float32
        )
        return (
            context.reshape(S, D).astype(jnp.bfloat16),
            (peak_score + jnp.log(sum_total))[..., 0],
        )

    attended_rows, log_totals = lax.map(attend, (qkv_rows, segments))
    attended = attended_rows.reshape(local_rows, D)
    branch = jnp.dot(attended, out_weight, preferred_element_type=jnp.float32) + out_bias.astype(
        jnp.float32
    )
    first_norm, norm_one_back = jax.vjp(
        layer_norm,
        tokens.astype(jnp.float32) + branch,
        gain_one.astype(jnp.float32),
        shift_one.astype(jnp.float32),
    )
    first_low = first_norm.astype(jnp.bfloat16)
    hidden_pre = jnp.einsum(
        "rd,zdf->zrf", first_low, up_all, preferred_element_type=jnp.float32
    ) + up_bias_all.astype(jnp.float32)[:, None]
    hidden, gelu_back = jax.vjp(gelu_exact, hidden_pre)
    hidden = hidden.astype(jnp.bfloat16)
    feed_out = jnp.einsum(
        "zrf,zfd->rd", hidden, down_all, preferred_element_type=jnp.float32
    ) + down_bias.astype(jnp.float32)
    output, norm_two_back = jax.vjp(
        layer_norm,
        first_norm + feed_out,
        gain_two.astype(jnp.float32),
        shift_two.astype(jnp.float32),
    )
    grad_second, grad_gain_two, grad_shift_two = norm_two_back(cotangent.astype(jnp.float32))
    grad_feed = grad_second.astype(jnp.bfloat16)
    grad_down_bias = jnp.sum(grad_feed, axis=0, dtype=jnp.float32)
    grad_down = jnp.einsum("zrf,rd->zfd", hidden, grad_feed, preferred_element_type=jnp.float32)
    grad_hidden = jnp.einsum(
        "rd,zfd->zrf", grad_feed, down_all, preferred_element_type=jnp.float32
    )
    grad_pre = gelu_back(grad_hidden)[0].astype(jnp.bfloat16)
    grad_up = jnp.einsum("rd,zrf->zdf", first_low, grad_pre, preferred_element_type=jnp.float32)
    grad_up_bias = jnp.sum(grad_pre, axis=1, dtype=jnp.float32)
    grad_first = grad_second + jnp.einsum(
        "zrf,zdf->rd", grad_pre, up_all, preferred_element_type=jnp.float32
    )

    feed_grads = jnp.stack([grad_up, grad_down]).astype(BF)
    feed_out_parts = []
    for g, order in enumerate(orders):
        block = feed_grads[:, :, g * third : (g + 1) * third]
        block = block.reshape([2] + tw + dw + [part, D])
        block = jnp.moveaxis(block, 0, len(tb) + len(db))
        own = ex.reduce(block, tb + db, order)
        back = [b for b in order[::-1] if b in ex.dp_bits]
        full = ex.gather(own, back)
        full = to_order(full, back[::-1], db).reshape(n_dp, 2, part, D)
        feed_out_parts.append(full.transpose(1, 0, 2, 3).reshape(2, third, D))
    feed_final = jnp.concatenate(feed_out_parts, axis=1).astype(F32)

    grad_resid, grad_gain_one, grad_shift_one = norm_one_back(grad_first)
    grad_branch = grad_resid.astype(jnp.bfloat16)
    grad_out_bias = jnp.sum(grad_branch, axis=0, dtype=jnp.float32)
    grad_out_weight = jnp.einsum(
        "rd,re->de", attended, grad_branch, preferred_element_type=jnp.float32
    )
    grad_attended = jnp.einsum(
        "re,de->rd", grad_branch, out_weight, preferred_element_type=jnp.float32
    ).astype(jnp.bfloat16)

    def attend_back(mask_carry, row_quad):
        row_block, segment_row, log_total, grad_context = row_quad
        scores, heads_view = row_scores(row_block, segment_row, mask_term)
        probabilities = jnp.exp(scores - log_total[..., None])
        weights = probabilities.astype(jnp.bfloat16)
        grad_heads = grad_context.reshape(S, H, HD)
        grad_weights = jnp.einsum(
            "qhd,khd->hqk", grad_heads, heads_view[:, 2], preferred_element_type=jnp.float32
        )
        centre = jnp.sum(grad_weights * probabilities, axis=-1, keepdims=True)
        grad_scores = (probabilities * (grad_weights - centre)).astype(jnp.bfloat16)
        grad_query = jnp.einsum(
            "hqk,khd->qhd", grad_scores, heads_view[:, 1], preferred_element_type=jnp.float32
        ) * HD ** (-0.5)
        grad_key = jnp.einsum(
            "hqk,qhd->khd", grad_scores, heads_view[:, 0], preferred_element_type=jnp.float32
        ) * HD ** (-0.5)
        grad_value = jnp.einsum(
            "hqk,qhd->khd", weights, grad_heads, preferred_element_type=jnp.float32
        )
        stacked = (
            jnp.stack([grad_query, grad_key, grad_value], axis=1)
            .reshape(S, 3 * D)
            .astype(jnp.bfloat16)
        )
        return (mask_carry + grad_scores.astype(jnp.float32), stacked)

    mask_start = jnp.zeros(mask_term.shape, jnp.float32)
    mask_total, grad_qkv_rows = lax.scan(
        attend_back,
        mask_start,
        (qkv_rows, segments, log_totals, grad_attended.reshape(row_count, S, D)),
    )
    heads = H // 3
    qs, ks = S // n_dp, S // n_tensor
    mask_low = mask_total.astype(BF).reshape(H, n_dp, qs, n_tensor, ks).transpose(1, 3, 0, 2, 4)
    mask_parts = []
    for g, order in enumerate(orders):
        block = mask_low[:, :, g * heads : (g + 1) * heads].reshape(dw + tw + [heads, qs, ks])
        mask_parts.append(ex.reduce(block, db + tb, order))
    mask_own = jnp.concatenate(mask_parts).astype(F32)

    def own_block(a):
        starts = (0, lax.axis_index("dp") * qs, lax.axis_index("tensor") * ks)
        return lax.dynamic_slice(a, starts, (H, qs, ks)).astype(F32)

    mask_grad = mask_own * jax.nn.sigmoid(-(own_block(mask_logits) + own_block(mask_noise)))

    grad_qkv = grad_qkv_rows.reshape(local_rows, 3 * D)
    grad_qkv_weight = jnp.einsum(
        "rd,rpc->pdc", tokens, grad_qkv.reshape(local_rows, 3, D), preferred_element_type=F32
    )
    whole_grads = jnp.concatenate([grad_qkv_weight, grad_out_weight[None]]).astype(BF)
    share = (4 * D) // 3 // ex.count
    whole_grads = whole_grads.reshape([3] + dw + tw + [share, D])
    whole_parts = []
    for g, order in enumerate(orders):
        own = ex.reduce(whole_grads[g], db + tb, order)
        full = ex.gather(own, order[::-1])
        whole_parts.append(to_order(full, order, db + tb).reshape(-1, D))
    whole_final = jnp.concatenate(whole_parts).reshape(4, D, D).astype(F32)
    qkv_final = whole_final[:3].transpose(1, 0, 2).reshape(D, 3 * D)

    bias_sums = jnp.sum(grad_qkv, axis=0, dtype=jnp.float32)
    grad_tokens = grad_resid + jnp.einsum(
        "rc,dc->rd", grad_qkv, qkv_weight, preferred_element_type=jnp.float32
    )
    vectors = jnp.concatenate(
        [
            bias_sums[:D],
            bias_sums[2 * D :],
            grad_out_bias,
            grad_gain_one,
            grad_shift_one,
            grad_down_bias,
            grad_gain_two,
            grad_shift_two,
            grad_up_bias.reshape(-1),
        ]
    )
    vectors = ex.total(vectors, orders[0])
    take = lambda at, n=D: vectors[at * D : at * D + n]
    up_bias_final = lax.dynamic_slice_in_dim(vectors, 8 * D + lax.axis_index("tensor") * fs, fs)
    return (
        output.astype(jnp.bfloat16),
        grad_tokens,
        qkv_final,
        take(0, 2 * D),
        whole_final[3],
        take(2),
        take(3),
        take(4),
        feed_final[0],
        up_bias_final,
        feed_final[1],
        take(5),
        take(6),
        take(7),
        mask_grad,
    )


def solution(mesh):
    rows = P(AXES, None)
    ins = (rows, rows) + (P(),) * 6
    ins += (P(None, "tensor"), P("tensor"), P("tensor", None)) + (P(),) * 5 + (rows,)
    outs = (rows, rows) + (P(),) * 6
    outs += (P(None, "tensor"), P("tensor"), P("tensor", None)) + (P(),) * 3
    outs += (P(None, "dp", "tensor"),)

    def step(*args):
        return local(*args, n_dp=mesh.shape["dp"], n_tensor=mesh.shape["tensor"])

    return jax.shard_map(step, mesh=mesh, in_specs=ins, out_specs=outs, check_vma=False)
```

```python
import functools

import jax
import jax.numpy as jnp
from jax import lax
from jax.experimental import pallas as pl
from jax.experimental.pallas import tpu as pltpu
from jax.sharding import PartitionSpec as P

D = 768
H = 12
HD = 64
S = 512
AXES = ("dp", "tensor")
BF = jnp.bfloat16
F32 = jnp.float32

epsilon = 1e-12
negative = -1e30


def layer_norm(values, gain_vec, shift_vec):
    average = jnp.mean(values, axis=-1, keepdims=True)
    centred = values - average
    variance = jnp.mean(centred * centred, axis=-1, keepdims=True)
    return centred * lax.rsqrt(variance + epsilon) * gain_vec + shift_vec


def gelu_with_slope(v):
    cdf = 0.5 + 0.5 * lax.erf(v * 0.5**0.5)
    return v * cdf, cdf + v * jnp.exp(-0.5 * v * v) * (0.5 / jnp.pi) ** 0.5


PAIR = 2 * HD
CHUNK = 256
GROUPS = 3
NT = (((1,), (1,)), ((), ()))


def dot(a, b):
    return jnp.dot(a, b, preferred_element_type=F32)


def dot_nt(a, b):
    return lax.dot_general(a, b, NT, preferred_element_type=F32)


def lanes_of(h, value=1.0):
    lane = lax.broadcasted_iota(jnp.int32, (1, PAIR), 1)
    return jnp.where(lane // HD == h, value, 0.0).astype(F32)


def attend_kernel(q_ref, k_ref, v_ref, sq_ref, sk_ref, ml_ref, mn_ref, o_ref, p_ref, term_ref):
    @pl.when(pl.program_id(1) == 0)
    def _():
        for h in range(2):
            total = ml_ref[h].astype(F32) + mn_ref[h].astype(F32)
            term_ref[h] = jnp.minimum(total, 0.0) - jnp.log(1.0 + jnp.exp(-jnp.abs(total)))

    first = lax.broadcasted_iota(jnp.int32, (CHUNK, PAIR), 1) < HD
    keys, values = k_ref[...], v_ref[...]
    for c in range(S // CHUNK):
        at = slice(c * CHUNK, (c + 1) * CHUNK)
        away = jnp.where(sq_ref[at, :1] == sk_ref[0], 0.0, negative)
        out = []
        for h in range(2):
            mine = (q_ref[at].astype(F32) * lanes_of(h, HD ** (-0.5))).astype(BF)
            scores = dot_nt(mine, keys) + (term_ref[h, at] + away)
            expo = jnp.exp(scores - jnp.max(scores, axis=1, keepdims=True))
            weights = (expo * (1.0 / jnp.sum(expo, axis=1, keepdims=True))).astype(BF)
            p_ref[0, h, at] = weights
            out.append(dot(weights, values))
        o_ref[at] = jnp.where(first, out[0], out[1]).astype(BF)


def attend(qkv, segments, mask_logits, mask_noise):
    tokens, rows = qkv.shape[0], segments.shape[0]
    pairs = H // 2
    column = lambda part: pl.BlockSpec((S, PAIR), lambda p, r: (r, part * pairs + p))
    heads = pl.BlockSpec((2, S, S), lambda p, r: (p, 0, 0))
    seg_q = jnp.broadcast_to(segments.reshape(tokens, 1), (tokens, 128))
    return pl.pallas_call(
        attend_kernel,
        name="attend",
        grid=(pairs, rows),
        in_specs=[
            column(0),
            column(1),
            column(2),
            pl.BlockSpec((S, 128), lambda p, r: (r, 0)),
            pl.BlockSpec((1, 1, S), lambda p, r: (r, 0, 0)),
            heads,
            heads,
        ],
        out_specs=[
            pl.BlockSpec((S, PAIR), lambda p, r: (r, p)),
            pl.BlockSpec((1, 2, S, S), lambda p, r: (r, p, 0, 0)),
        ],
        out_shape=[
            jax.ShapeDtypeStruct((tokens, D), BF),
            jax.ShapeDtypeStruct((rows, H, S, S), BF),
        ],
        scratch_shapes=[pltpu.VMEM((2, S, S), F32)],
        cost_estimate=pl.CostEstimate(
            flops=rows * H * S * S * HD * 8, bytes_accessed=rows * H * S * S * 4, transcendentals=rows * H * S * S
        ),
    )(qkv, qkv, qkv, seg_q, segments.reshape(rows, 1, S), mask_logits, mask_noise)


def attend_back_kernel(rows, n_dp, n_tensor, q_ref, k_ref, v_ref, g_ref, p_ref, d_ref, m_ref):
    step = pl.program_id(0)
    pairs = pl.num_programs(0)
    qs, ks = S // n_dp, S // n_tensor
    first = lax.broadcasted_iota(jnp.int32, (CHUNK, PAIR), 1) < HD
    chunks = S // CHUNK
    mask_sum = [[None] * chunks for _ in range(2)]
    for r in range(rows):
        row = slice(r * S, (r + 1) * S)
        keys, values = k_ref[row], v_ref[row]
        q_cols = q_ref[row].astype(F32).T.astype(BF)
        g_cols = g_ref[row].astype(F32).T.astype(BF)
        key_rows, value_rows = [], []
        query_out = [[None] * 2 for _ in range(chunks)]
        for h in range(2):
            cols = slice(h * HD, (h + 1) * HD)
            d_key = d_value = None
            for c in range(chunks):
                at = slice(c * CHUNK, (c + 1) * CHUNK)
                here = slice(r * S + c * CHUNK, r * S + (c + 1) * CHUNK)
                grad = (g_ref[here].astype(F32) * lanes_of(h)).astype(BF)
                weights = p_ref[r, h, at]
                probs = weights.astype(F32)
                inner = dot_nt(grad, values)
                centre = jnp.sum(inner * probs, axis=1, keepdims=True)
                grad_scores = (probs * (inner - centre)).astype(BF)
                if r == 0:
                    mask_sum[h][c] = grad_scores.astype(F32)
                else:
                    mask_sum[h][c] = mask_sum[h][c] + grad_scores.astype(F32)
                query_out[c][h] = dot(grad_scores, keys)
                part_key = dot(q_cols[cols, at], grad_scores)
                part_value = dot(g_cols[cols, at], weights)
                d_key = part_key if c == 0 else d_key + part_key
                d_value = part_value if c == 0 else d_value + part_value
            key_rows.append(d_key)
            value_rows.append(d_value)
        scale = HD ** (-0.5)
        for c in range(chunks):
            here = slice(r * S + c * CHUNK, r * S + (c + 1) * CHUNK)
            merged = jnp.where(first, query_out[c][0], query_out[c][1]) * scale
            d_ref[here, pl.ds(pl.multiple_of(step * PAIR, PAIR), PAIR)] = merged.astype(BF)
        for part, blocks, factor in ((1, key_rows, scale), (2, value_rows, 1.0)):
            merged = (jnp.concatenate(blocks, axis=0) * factor).T
            d_ref[row, pl.ds(pl.multiple_of((part * pairs + step) * PAIR, PAIR), PAIR)] = merged.astype(BF)
    for h in range(2):
        for c in range(chunks):
            low = mask_sum[h][c].astype(BF)
            for i in range(n_dp // chunks):
                for j in range(n_tensor):
                    m_ref[c * (n_dp // chunks) + i, j, h] = low[i * qs : (i + 1) * qs, j * ks : (j + 1) * ks]


def attend_back(group, qkv, grads, weights, n_dp, n_tensor):
    tokens, rows = qkv.shape[0], weights.shape[0]
    pairs = H // 2
    own = pairs // GROUPS
    column = lambda part: pl.BlockSpec((tokens, PAIR), lambda p: (0, part * pairs + group * own + p))
    qs, ks = S // n_dp, S // n_tensor
    return pl.pallas_call(
        functools.partial(attend_back_kernel, rows, n_dp, n_tensor),
        name="attend_back",
        grid=(own,),
        in_specs=[
            column(0),
            column(1),
            column(2),
            column(0),
            pl.BlockSpec((rows, 2, S, S), lambda p: (0, group * own + p, 0, 0)),
        ],
        out_specs=[
            pl.BlockSpec((tokens, 3 * own * PAIR), lambda p: (0, 0)),
            pl.BlockSpec((n_dp, n_tensor, 2, qs, ks), lambda p: (0, 0, p, 0, 0)),
        ],
        out_shape=[
            jax.ShapeDtypeStruct((tokens, 3 * own * PAIR), BF),
            jax.ShapeDtypeStruct((n_dp, n_tensor, 2 * own, qs, ks), BF),
        ],
        cost_estimate=pl.CostEstimate(
            flops=rows * 2 * own * S * S * HD * 16, bytes_accessed=rows * 2 * own * S * S * 3, transcendentals=0
        ),
    )(qkv, qkv, qkv, grads, weights)


class Exchange:
    def __init__(self, n_dp, n_tensor):
        self.count = n_dp * n_tensor
        self.tensor_bits = list(range(n_tensor.bit_length() - 1))
        first = len(self.tensor_bits)
        self.dp_bits = list(range(first, first + n_dp.bit_length() - 1))
        self.index = lax.axis_index("dp") * n_tensor + lax.axis_index("tensor")

    def orders(self):
        near, rest = self.dp_bits[0], self.dp_bits[1:]
        low, high = self.tensor_bits[:1], self.tensor_bits[1:]
        return (
            [near] + rest + low + high,
            [near] + rest[1:] + low + rest[:1] + high,
            [near] + low + rest + high,
        )

    def bit(self, b):
        return (self.index >> b) & 1

    def swap(self, x, b):
        return lax.ppermute(x, AXES, [(i, i ^ (1 << b)) for i in range(self.count)])

    def reduce(self, x, axes, order):
        axes = list(axes)
        for b in order:
            at = axes.index(b)
            mine = self.bit(b)
            sent = lax.dynamic_index_in_dim(x, 1 - mine, at, keepdims=False).astype(BF)
            kept = lax.dynamic_index_in_dim(x, mine, at, keepdims=False)
            got = self.swap(sent, b)
            x = (kept.astype(F32) + got.astype(F32)).astype(BF)
            axes.pop(at)
        return x

    def gather(self, x, order):
        for b in order:
            got = self.swap(x, b)
            mine = self.bit(b) == 1
            x = jnp.stack([jnp.where(mine, got, x), jnp.where(mine, x, got)])
        return x

    def total(self, x, order):
        for b in order:
            x = x + self.swap(x, b)
        return x


def to_order(x, have, want):
    n = len(have)
    return jnp.transpose(x, [have.index(b) for b in want] + list(range(n, x.ndim)))


def local(
    tokens,
    segments,
    qkv_weight,
    qv_bias,
    out_weight,
    out_bias,
    gain_one,
    shift_one,
    up_weight,
    up_bias,
    down_weight,
    down_bias,
    gain_two,
    shift_two,
    mask_logits,
    mask_noise,
    cotangent,
    *,
    n_dp,
    n_tensor,
):
    ex = Exchange(n_dp, n_tensor)
    orders = ex.orders()
    tb, db = ex.tensor_bits[::-1], ex.dp_bits[::-1]
    tw, dw = [2] * len(tb), [2] * len(db)
    fs = up_weight.shape[1]
    dp_at = lax.axis_index("dp")

    third = D // 3
    part = third // n_dp
    gathered = []
    for g, order in enumerate(orders):
        mine = jnp.stack(
            [
                lax.dynamic_slice_in_dim(up_weight, g * third + dp_at * part, part, 0),
                lax.dynamic_slice_in_dim(down_weight, g * third + dp_at * part, part, 0),
            ]
        )
        full = ex.gather(mine, order[::-1])
        full = to_order(full, order, tb + db)
        full = full.reshape((n_tensor, n_dp, 2, part, D))
        gathered.append(full.transpose(2, 0, 1, 3, 4).reshape(2, n_tensor, third, D))
    weights_all = jnp.concatenate(gathered, axis=2)
    up_all, down_all = weights_all[0], weights_all[1]
    up_bias_all = ex.gather(up_bias, ex.tensor_bits).reshape(n_tensor, fs)

    qv_float = qv_bias.astype(jnp.float32)
    full_bias = jnp.concatenate([qv_float[:D], jnp.zeros((D,), jnp.float32), qv_float[D:]])
    projected = jnp.dot(tokens, qkv_weight, preferred_element_type=jnp.float32) + full_bias
    qkv = projected.astype(BF)
    attended, weights = attend(qkv, segments, mask_logits, mask_noise)
    branch = jnp.dot(attended, out_weight, preferred_element_type=jnp.float32) + out_bias.astype(
        jnp.float32
    )
    first_norm, norm_one_back = jax.vjp(
        layer_norm,
        tokens.astype(jnp.float32) + branch,
        gain_one.astype(jnp.float32),
        shift_one.astype(jnp.float32),
    )
    first_low = first_norm.astype(jnp.bfloat16)
    hidden_pre = jnp.einsum(
        "rd,zdf->zrf", first_low, up_all, preferred_element_type=jnp.float32
    ) + up_bias_all.astype(jnp.float32)[:, None]
    hidden, slope = gelu_with_slope(hidden_pre)
    hidden, slope = hidden.astype(BF), slope.astype(BF)
    feed_out = jnp.einsum(
        "zrf,zfd->rd", hidden, down_all, preferred_element_type=jnp.float32
    ) + down_bias.astype(jnp.float32)
    output, norm_two_back = jax.vjp(
        layer_norm,
        first_norm + feed_out,
        gain_two.astype(jnp.float32),
        shift_two.astype(jnp.float32),
    )
    grad_second, grad_gain_two, grad_shift_two = norm_two_back(cotangent.astype(jnp.float32))
    grad_feed = grad_second.astype(jnp.bfloat16)
    grad_down_bias = jnp.sum(grad_feed, axis=0, dtype=jnp.float32)
    grad_down = jnp.einsum("zrf,rd->zfd", hidden, grad_feed, preferred_element_type=jnp.float32)
    grad_hidden = jnp.einsum(
        "rd,zfd->zrf", grad_feed, down_all, preferred_element_type=jnp.float32
    )
    grad_pre = (grad_hidden * slope.astype(F32)).astype(BF)
    grad_up = jnp.einsum("rd,zrf->zdf", first_low, grad_pre, preferred_element_type=jnp.float32)
    grad_up_bias = jnp.sum(grad_pre, axis=1, dtype=jnp.float32)
    grad_first = grad_second + jnp.einsum(
        "zrf,zdf->rd", grad_pre, up_all, preferred_element_type=jnp.float32
    )

    feed_grads = jnp.stack([grad_up, grad_down]).astype(BF)
    feed_out_parts = []
    for g, order in enumerate(orders):
        block = feed_grads[:, :, g * third : (g + 1) * third]
        block = block.reshape([2] + tw + dw + [part, D])
        block = jnp.moveaxis(block, 0, len(tb) + len(db))
        own = ex.reduce(block, tb + db, order)
        back = [b for b in order[::-1] if b in ex.dp_bits]
        full = ex.gather(own, back)
        full = to_order(full, back[::-1], db).reshape(n_dp, 2, part, D)
        feed_out_parts.append(full.transpose(1, 0, 2, 3).reshape(2, third, D))
    feed_final = jnp.concatenate(feed_out_parts, axis=1).astype(F32)

    grad_resid, grad_gain_one, grad_shift_one = norm_one_back(grad_first)
    grad_branch = grad_resid.astype(jnp.bfloat16)
    grad_out_bias = jnp.sum(grad_branch, axis=0, dtype=jnp.float32)
    grad_out_weight = jnp.einsum(
        "rd,re->de", attended, grad_branch, preferred_element_type=jnp.float32
    )
    grad_attended = jnp.einsum(
        "re,de->rd", grad_branch, out_weight, preferred_element_type=jnp.float32
    ).astype(jnp.bfloat16)

    cut = D // GROUPS
    pick = lambda a, g: jnp.concatenate(
        [a[..., p * D + g * cut : p * D + (g + 1) * cut] for p in range(3)], axis=-1
    )
    mask_parts, whole_parts, bias_parts = [], [], []
    grad_tokens = grad_resid
    rows_each = (D + cut) // ex.count
    for g, order in enumerate(orders):
        grad_cols, mask_low = attend_back(g, qkv, grad_attended, weights, n_dp, n_tensor)
        block = mask_low.reshape(dw + tw + list(mask_low.shape[2:]))
        mask_parts.append(ex.reduce(block, db + tb, order))
        grad_weight = jnp.einsum("rd,rc->dc", tokens, grad_cols, preferred_element_type=F32)
        both = jnp.concatenate([grad_weight, grad_out_weight[g * cut : (g + 1) * cut]]).astype(BF)
        both = both.reshape(dw + tw + [rows_each, D])
        full = ex.gather(ex.reduce(both, db + tb, order), order[::-1])
        whole_parts.append(to_order(full, order, db + tb).reshape(D + cut, D))
        bias_parts.append(jnp.sum(grad_cols, axis=0, dtype=F32).reshape(3, cut))
        grad_tokens = grad_tokens + jnp.einsum(
            "rc,dc->rd", grad_cols, pick(qkv_weight, g), preferred_element_type=F32
        )
    mask_own = jnp.concatenate(mask_parts).astype(F32)
    qs, ks = S // n_dp, S // n_tensor

    def own_block(a):
        starts = (0, lax.axis_index("dp") * qs, lax.axis_index("tensor") * ks)
        return lax.dynamic_slice(a, starts, (H, qs, ks)).astype(F32)

    mask_grad = mask_own * jax.nn.sigmoid(-(own_block(mask_logits) + own_block(mask_noise)))

    qkv_final = jnp.stack([w[:D].reshape(D, 3, cut) for w in whole_parts], axis=2)
    qkv_final = qkv_final.reshape(D, 3 * D).astype(F32)
    out_final = jnp.concatenate([w[D:] for w in whole_parts]).astype(F32)
    bias_sums = jnp.stack(bias_parts, axis=1).reshape(3 * D)
    vectors = jnp.concatenate(
        [
            bias_sums[:D],
            bias_sums[2 * D :],
            grad_out_bias,
            grad_gain_one,
            grad_shift_one,
            grad_down_bias,
            grad_gain_two,
            grad_shift_two,
            grad_up_bias.reshape(-1),
        ]
    )
    vectors = ex.total(vectors, orders[0])
    take = lambda at, n=D: vectors[at * D : at * D + n]
    up_bias_final = lax.dynamic_slice_in_dim(vectors, 8 * D + lax.axis_index("tensor") * fs, fs)
    return (
        output.astype(jnp.bfloat16),
        grad_tokens,
        qkv_final,
        take(0, 2 * D),
        out_final,
        take(2),
        take(3),
        take(4),
        feed_final[0],
        up_bias_final,
        feed_final[1],
        take(5),
        take(6),
        take(7),
        mask_grad,
    )


def solution(mesh):
    rows = P(AXES, None)
    ins = (rows, rows) + (P(),) * 6
    ins += (P(None, "tensor"), P("tensor"), P("tensor", None)) + (P(),) * 5 + (rows,)
    outs = (rows, rows) + (P(),) * 6
    outs += (P(None, "tensor"), P("tensor"), P("tensor", None)) + (P(),) * 3
    outs += (P(None, "dp", "tensor"),)

    def step(*args):
        return local(*args, n_dp=mesh.shape["dp"], n_tensor=mesh.shape["tensor"])

    return jax.shard_map(step, mesh=mesh, in_specs=ins, out_specs=outs, check_vma=False)
```

```python
import functools

import jax
import jax.numpy as jnp
from jax import lax
from jax.experimental import pallas as pl
from jax.experimental.pallas import tpu as pltpu

from jax.sharding import PartitionSpec as P

D = 768
H = 12
HD = 64
S = 512
AXES = ("dp", "tensor")
BF = jnp.bfloat16
F32 = jnp.float32


epsilon = 1e-12
negative = -1e30


def layer_norm(values, gain_vec, shift_vec):
    average = jnp.mean(values, axis=-1, keepdims=True)
    centred = values - average
    variance = jnp.mean(centred * centred, axis=-1, keepdims=True)
    return centred * lax.rsqrt(variance + epsilon) * gain_vec + shift_vec


def gelu_with_slope(v):
    cdf = 0.5 + 0.5 * lax.erf(v * 0.5**0.5)
    return v * cdf, cdf + v * jnp.exp(-0.5 * v * v) * (0.5 / jnp.pi) ** 0.5


PAIR = 2 * HD
CHUNK = 256
GROUPS = 3
NT = (((1,), (1,)), ((), ()))


def dot(a, b):
    return jnp.dot(a, b, preferred_element_type=F32)


def dot_nt(a, b):
    return lax.dot_general(a, b, NT, preferred_element_type=F32)


def lanes_of(h, value=1.0):
    lane = lax.broadcasted_iota(jnp.int32, (1, PAIR), 1)
    return jnp.where(lane // HD == h, value, 0.0).astype(F32)


def attend_kernel(q_ref, k_ref, v_ref, sq_ref, sk_ref, ml_ref, mn_ref, o_ref, p_ref, term_ref):
    @pl.when(pl.program_id(1) == 0)
    def _():
        for h in range(2):
            total = ml_ref[h].astype(F32) + mn_ref[h].astype(F32)
            term_ref[h] = jnp.minimum(total, 0.0) - jnp.log(1.0 + jnp.exp(-jnp.abs(total)))

    first = lax.broadcasted_iota(jnp.int32, (CHUNK, PAIR), 1) < HD
    keys, values = k_ref[...], v_ref[...]
    for c in range(S // CHUNK):
        at = slice(c * CHUNK, (c + 1) * CHUNK)
        away = jnp.where(sq_ref[at, :1] == sk_ref[0], 0.0, negative)
        out = []
        for h in range(2):
            mine = (q_ref[at].astype(F32) * lanes_of(h, HD ** (-0.5))).astype(BF)
            scores = dot_nt(mine, keys) + (term_ref[h, at] + away)
            expo = jnp.exp(scores - jnp.max(scores, axis=1, keepdims=True))
            weights = (expo * (1.0 / jnp.sum(expo, axis=1, keepdims=True))).astype(BF)
            p_ref[0, h, at] = weights
            out.append(dot(weights, values))
        o_ref[at] = jnp.where(first, out[0], out[1]).astype(BF)


def attend(group, qkv, seg_q, segments, mask_logits, mask_noise):
    tokens, rows = qkv.shape[0], segments.shape[0]
    pairs = H // 2
    own = pairs // GROUPS
    column = lambda part: pl.BlockSpec((S, PAIR), lambda p, r: (r, part * pairs + group * own + p))
    heads = pl.BlockSpec((2, S, S), lambda p, r: (group * own + p, 0, 0))
    return pl.pallas_call(
        attend_kernel,
        name="attend",
        grid=(own, rows),
        in_specs=[
            column(0),
            column(1),
            column(2),
            pl.BlockSpec((S, 128), lambda p, r: (r, 0)),
            pl.BlockSpec((1, 1, S), lambda p, r: (r, 0, 0)),
            heads,
            heads,
        ],
        out_specs=[
            pl.BlockSpec((S, PAIR), lambda p, r: (r, p)),
            pl.BlockSpec((1, 2, S, S), lambda p, r: (r, p, 0, 0)),
        ],
        out_shape=[
            jax.ShapeDtypeStruct((tokens, own * PAIR), BF),
            jax.ShapeDtypeStruct((rows, 2 * own, S, S), BF),
        ],
        scratch_shapes=[pltpu.VMEM((2, S, S), F32)],
        cost_estimate=pl.CostEstimate(
            flops=rows * 2 * own * S * S * HD * 8,
            bytes_accessed=rows * 2 * own * S * S * 4,
            transcendentals=rows * 2 * own * S * S,
        ),
    )(qkv, qkv, qkv, seg_q, segments.reshape(rows, 1, S), mask_logits, mask_noise)


def attend_back_kernel(rows, n_dp, n_tensor, q_ref, k_ref, v_ref, g_ref, p_ref, d_ref, b_ref, m_ref):
    step = pl.program_id(0)
    pairs = pl.num_programs(0)
    qs, ks = S // n_dp, S // n_tensor
    first = lax.broadcasted_iota(jnp.int32, (CHUNK, PAIR), 1) < HD
    chunks = S // CHUNK
    mask_sum = [[None] * chunks for _ in range(2)]
    bias_sums = [jnp.zeros((1, PAIR), F32)] * 2
    for r in range(rows):
        row = slice(r * S, (r + 1) * S)
        keys, values = k_ref[row], v_ref[row]
        q_cols = q_ref[row].astype(F32).T.astype(BF)
        g_cols = g_ref[row].astype(F32).T.astype(BF)
        key_rows, value_rows = [], []
        query_out = [[None] * 2 for _ in range(chunks)]
        for h in range(2):
            cols = slice(h * HD, (h + 1) * HD)
            d_key = d_value = None
            for c in range(chunks):
                at = slice(c * CHUNK, (c + 1) * CHUNK)
                here = slice(r * S + c * CHUNK, r * S + (c + 1) * CHUNK)
                grad = (g_ref[here].astype(F32) * lanes_of(h)).astype(BF)
                weights = p_ref[r, h, at]
                probs = weights.astype(F32)
                inner = dot_nt(grad, values)
                centre = jnp.sum(inner * probs, axis=1, keepdims=True)
                grad_scores = (probs * (inner - centre)).astype(BF)
                if r == 0:
                    mask_sum[h][c] = grad_scores.astype(F32)
                else:
                    mask_sum[h][c] = mask_sum[h][c] + grad_scores.astype(F32)
                query_out[c][h] = dot(grad_scores, keys)
                part_key = dot(q_cols[cols, at], grad_scores)
                part_value = dot(g_cols[cols, at], weights)
                d_key = part_key if c == 0 else d_key + part_key
                d_value = part_value if c == 0 else d_value + part_value
            key_rows.append(d_key)
            value_rows.append(d_value)
        scale = HD ** (-0.5)
        for c in range(chunks):
            here = slice(r * S + c * CHUNK, r * S + (c + 1) * CHUNK)
            merged = jnp.where(first, query_out[c][0], query_out[c][1]) * scale
            d_ref[here, pl.ds(pl.multiple_of(step * PAIR, PAIR), PAIR)] = merged.astype(BF)
            bias_sums[0] = bias_sums[0] + jnp.sum(merged.astype(BF).astype(F32), axis=0, keepdims=True)
        for part, blocks, factor in ((1, key_rows, scale), (2, value_rows, 1.0)):
            merged = (jnp.concatenate(blocks, axis=0) * factor).T
            d_ref[row, pl.ds(pl.multiple_of((part * pairs + step) * PAIR, PAIR), PAIR)] = merged.astype(BF)
            if part == 2:
                bias_sums[1] = bias_sums[1] + jnp.sum(merged.astype(BF).astype(F32), axis=0, keepdims=True)
    for i in range(2):
        b_ref[i] = jnp.broadcast_to(bias_sums[i], (8, PAIR))
    for h in range(2):
        for c in range(chunks):
            low = mask_sum[h][c].astype(BF)
            for i in range(n_dp // chunks):
                for j in range(n_tensor):
                    m_ref[c * (n_dp // chunks) + i, j, h] = low[i * qs : (i + 1) * qs, j * ks : (j + 1) * ks]


def attend_back(group, qkv, grads, weights, n_dp, n_tensor):
    tokens, rows = qkv.shape[0], weights.shape[0]
    pairs = H // 2
    own = pairs // GROUPS
    column = lambda part: pl.BlockSpec((tokens, PAIR), lambda p: (0, part * pairs + group * own + p))
    qs, ks = S // n_dp, S // n_tensor
    return pl.pallas_call(
        functools.partial(attend_back_kernel, rows, n_dp, n_tensor),
        name="attend_back",
        grid=(own,),
        in_specs=[
            column(0),
            column(1),
            column(2),
            column(0),
            pl.BlockSpec((rows, 2, S, S), lambda p: (0, p, 0, 0)),
        ],
        out_specs=[
            pl.BlockSpec((tokens, 3 * own * PAIR), lambda p: (0, 0)),
            pl.BlockSpec((2, 8, PAIR), lambda p: (0, 0, p)),
            pl.BlockSpec((n_dp, n_tensor, 2, qs, ks), lambda p: (0, 0, p, 0, 0)),
        ],
        out_shape=[
            jax.ShapeDtypeStruct((tokens, 3 * own * PAIR), BF),
            jax.ShapeDtypeStruct((2, 8, own * PAIR), F32),
            jax.ShapeDtypeStruct((n_dp, n_tensor, 2 * own, qs, ks), BF),
        ],
        cost_estimate=pl.CostEstimate(
            flops=rows * 2 * own * S * S * HD * 16, bytes_accessed=rows * 2 * own * S * S * 3, transcendentals=0
        ),
    )(qkv, qkv, qkv, grads, weights)


class Exchange:
    def __init__(self, n_dp, n_tensor):
        self.count = n_dp * n_tensor
        self.tensor_bits = list(range(n_tensor.bit_length() - 1))
        first = len(self.tensor_bits)
        self.dp_bits = list(range(first, first + n_dp.bit_length() - 1))
        self.index = lax.axis_index("dp") * n_tensor + lax.axis_index("tensor")

    def orders(self):
        near, rest = self.dp_bits[0], self.dp_bits[1:]
        low, high = self.tensor_bits[:1], self.tensor_bits[1:]
        return (
            [near] + rest + low + high,
            [near] + rest[1:] + low + rest[:1] + high,
            [near] + low + rest + high,
        )

    def bit(self, b):
        return (self.index >> b) & 1

    def swap(self, x, b):
        return lax.ppermute(x, AXES, [(i, i ^ (1 << b)) for i in range(self.count)])

    def split(self, x, b, at, relative):
        pick = functools.partial(lax.dynamic_index_in_dim, x, axis=at, keepdims=False)
        if relative:
            return lax.index_in_dim(x, 1, at, False), lax.index_in_dim(x, 0, at, False)
        return pick(1 - self.bit(b)), pick(self.bit(b))

    def reduce(self, x, axes, order, relative=False):
        axes = list(axes)
        for b in order:
            at = axes.index(b)
            sent, kept = self.split(x, b, at, relative)
            got = self.swap(sent, b)
            x = (kept.astype(F32) + got.astype(F32)).astype(BF)
            axes.pop(at)
        return x

    def gather(self, x, order, axes, relative=False):
        held = []
        for b in order:
            got = self.swap(x, b)
            at = sum(axes.index(other) < axes.index(b) for other in held)
            if relative:
                x = jnp.stack([x, got], axis=at)
            else:
                mine = self.bit(b) == 1
                x = jnp.stack([jnp.where(mine, got, x), jnp.where(mine, x, got)], axis=at)
            held.append(b)
        return x

    def turn(self, x, axes):
        for at, b in enumerate(axes):
            x = jnp.where(self.bit(b) == 1, jnp.flip(x, at), x)
        return x


def local(
    tokens,
    segments,
    qkv_weight,
    qv_bias,
    out_weight,
    out_bias,
    gain_one,
    shift_one,
    up_weight,
    up_bias,
    down_weight,
    down_bias,
    gain_two,
    shift_two,
    mask_logits,
    mask_noise,
    cotangent,
    *,
    n_dp,
    n_tensor,
):
    ex = Exchange(n_dp, n_tensor)
    orders = ex.orders()
    tb, db = ex.tensor_bits[::-1], ex.dp_bits[::-1]
    tw, dw = [2] * len(tb), [2] * len(db)
    fs = up_weight.shape[1]
    part = fs // n_dp
    part_at = lax.axis_index("dp") * part
    near_first = ex.dp_bits + ex.tensor_bits[::-1]
    full_bits = [2] * len(near_first)

    up_share = lax.dynamic_slice_in_dim(up_weight, part_at, part, 1).T
    up_all = ex.gather(up_share, orders[1][::-1], near_first, True).reshape(-1, D)
    down_share = lax.dynamic_slice_in_dim(down_weight, part_at, part, 0)
    down_all = ex.gather(down_share, orders[0][::-1], near_first, True).reshape(-1, D)
    bias_bits = ex.gather(up_bias, ex.tensor_bits, tb, True).reshape(tw + dw + [part])
    bias_bits = jnp.moveaxis(bias_bits, range(len(tb)), range(-1 - len(tb), -1))
    bias_bits = ex.turn(bias_bits, db)
    bias_all = jnp.transpose(
        bias_bits, [(db + tb).index(b) for b in near_first] + [len(near_first)]
    ).reshape(-1)

    qv_float = qv_bias.astype(jnp.float32)
    full_bias = jnp.concatenate([qv_float[:D], jnp.zeros((D,), jnp.float32), qv_float[D:]])
    qkv = (dot(tokens, qkv_weight) + full_bias).astype(BF)
    seg_q = jnp.broadcast_to(segments.reshape(-1, 1), (tokens.shape[0], 128))
    attended_parts, weights = [], []
    for g in range(GROUPS):
        own_out, own_weights = attend(g, qkv, seg_q, segments, mask_logits, mask_noise)
        attended_parts.append(own_out)
        weights.append(own_weights)
    attended = jnp.concatenate(attended_parts, axis=1)
    branch = dot(attended, out_weight) + out_bias.astype(F32)
    first_norm, norm_one_back = jax.vjp(
        layer_norm,
        tokens.astype(jnp.float32) + branch,
        gain_one.astype(jnp.float32),
        shift_one.astype(jnp.float32),
    )
    first_low = first_norm.astype(jnp.bfloat16)
    hidden_pre = dot_nt(first_low, up_all) + bias_all.astype(F32)
    hidden, slope = gelu_with_slope(hidden_pre)
    hidden, slope = hidden.astype(BF), slope.astype(BF)
    feed_out = dot(hidden, down_all) + down_bias.astype(F32)
    output, norm_two_back = jax.vjp(
        layer_norm,
        first_norm + feed_out,
        gain_two.astype(jnp.float32),
        shift_two.astype(jnp.float32),
    )
    grad_second, grad_gain_two, grad_shift_two = norm_two_back(cotangent.astype(jnp.float32))
    grad_feed = grad_second.astype(jnp.bfloat16)
    grad_down_bias = jnp.sum(grad_feed, axis=0, dtype=jnp.float32)
    grad_down = jnp.einsum("rf,rd->fd", hidden, grad_feed, preferred_element_type=F32).astype(BF)
    grad_down = grad_down.reshape(full_bits + [part, D])
    down_own = ex.reduce(grad_down, near_first, orders[0], True)
    grad_pre = (dot_nt(grad_feed, down_all) * slope.astype(F32)).astype(BF)
    grad_up = jnp.einsum("rf,rd->fd", grad_pre, first_low, preferred_element_type=F32).astype(BF)
    grad_up = grad_up.reshape(full_bits + [part, D])
    up_own = ex.reduce(grad_up, near_first, orders[1], True)
    grad_up_bias = jnp.sum(grad_pre, axis=0, dtype=F32).reshape(full_bits + [part])
    grad_up_bias = jnp.transpose(
        ex.turn(grad_up_bias, near_first),
        [near_first.index(b) for b in tb + db] + [len(near_first)],
    ).reshape(-1)
    grad_first = grad_second + dot(grad_pre, up_all)
    feed_own = jnp.stack([up_own, down_own])
    back = [b for b in orders[0][::-1] if b in ex.dp_bits]
    feed_all = ex.gather(feed_own, back, db).reshape(n_dp, 2, part, D)
    up_final = feed_all[:, 0].reshape(fs, D).T.astype(F32)
    down_final = feed_all[:, 1].reshape(fs, D).astype(F32)

    grad_resid, grad_gain_one, grad_shift_one = norm_one_back(grad_first)
    grad_branch = grad_resid.astype(jnp.bfloat16)
    grad_out_bias = jnp.sum(grad_branch, axis=0, dtype=jnp.float32)
    grad_out_weight = jnp.einsum(
        "rd,re->de", attended, grad_branch, preferred_element_type=jnp.float32
    )
    grad_attended = jnp.einsum(
        "re,de->rd", grad_branch, out_weight, preferred_element_type=jnp.float32
    ).astype(jnp.bfloat16)

    cut = D // GROUPS
    pick = lambda a, g: jnp.concatenate(
        [a[..., p * D + g * cut : p * D + (g + 1) * cut] for p in range(3)], axis=-1
    )
    vectors = jnp.concatenate(
        [
            grad_out_bias,
            grad_gain_one,
            grad_shift_one,
            grad_down_bias,
            grad_gain_two,
            grad_shift_two,
            grad_up_bias,
        ]
    )
    piece = vectors.shape[0] // GROUPS
    each = (piece + 2 * cut) // ex.count
    mask_parts, weight_parts, vector_parts = [], [], []
    grad_tokens = grad_resid
    rows_each = (D + cut) // ex.count
    tiles = D // 128
    kept = rows_each * tiles
    for g in range(GROUPS):
        order = orders[(g + 2) % 3]
        grad_cols, bias_sums, mask_low = attend_back(g, qkv, grad_attended, weights[g], n_dp, n_tensor)
        grad_weight = jnp.einsum("rd,rc->dc", tokens, grad_cols, preferred_element_type=F32)
        grad_weight = grad_weight.astype(BF)
        out_rows = grad_out_weight[g * cut : (g + 1) * cut].astype(BF)
        both = jnp.concatenate([grad_weight, out_rows]).reshape(ex.count, rows_each, tiles, 128)
        both = both.transpose(0, 2, 1, 3).reshape(ex.count, kept, 128)
        small = jnp.concatenate(
            [bias_sums[:, 0].reshape(-1), vectors[g * piece : (g + 1) * piece]]
        ).reshape(ex.count, each)
        small = jnp.pad(small.astype(BF), ((0, 0), (0, 16 * 128 - each))).reshape(ex.count, 16, 128)
        mask_low = mask_low.reshape(ex.count, -1, 128)
        payload = jnp.concatenate([both, small, mask_low], axis=1)
        payload = payload.reshape(dw + tw + list(payload.shape[1:]))
        own = ex.reduce(payload, db + tb, order)
        mask_parts.append(own[kept + 16 :].reshape(H // GROUPS, S // n_dp, S // n_tensor))
        full = ex.gather(own[: kept + 16], order[::-1], db + tb)
        full = full.reshape(ex.count, kept + 16, 128)
        wide = full[:, :kept].reshape(ex.count, tiles, rows_each, 128).transpose(0, 2, 1, 3)
        weight_parts.append(wide.reshape(D + cut, D))
        vector_parts.append(full[:, kept:].reshape(ex.count, 16 * 128)[:, :each].reshape(-1))
        grad_tokens = grad_tokens + jnp.einsum(
            "rc,dc->rd", grad_cols, pick(qkv_weight, g), preferred_element_type=F32
        )
    mask_own = jnp.concatenate(mask_parts).astype(F32)
    qs, ks = S // n_dp, S // n_tensor

    def own_block(a):
        starts = (0, lax.axis_index("dp") * qs, lax.axis_index("tensor") * ks)
        return lax.dynamic_slice(a, starts, (H, qs, ks)).astype(F32)

    mask_grad = mask_own * jax.nn.sigmoid(-(own_block(mask_logits) + own_block(mask_noise)))

    qkv_final = jnp.stack([w[:D].reshape(D, 3, cut) for w in weight_parts], axis=2)
    qkv_final = qkv_final.reshape(D, 3 * D).astype(F32)
    out_final = jnp.concatenate([w[D:] for w in weight_parts]).astype(F32)
    bias_final = [v[p * cut : (p + 1) * cut] for p in range(2) for v in vector_parts]
    bias_final = jnp.concatenate(bias_final).astype(F32)
    vectors = jnp.concatenate([v[2 * cut :] for v in vector_parts]).astype(F32)
    take = lambda at: vectors[at * D : (at + 1) * D]
    up_bias_final = lax.dynamic_slice_in_dim(vectors, 6 * D + lax.axis_index("tensor") * fs, fs)
    return (
        output.astype(jnp.bfloat16),
        grad_tokens,
        qkv_final,
        bias_final,
        out_final,
        take(0),
        take(1),
        take(2),
        up_final,
        up_bias_final,
        down_final,
        take(3),
        take(4),
        take(5),
        mask_grad,
    )


def solution(mesh):
    rows = P(AXES, None)
    ins = (rows, rows) + (P(),) * 6
    ins += (P(None, "tensor"), P("tensor"), P("tensor", None)) + (P(),) * 5 + (rows,)
    outs = (rows, rows) + (P(),) * 6
    outs += (P(None, "tensor"), P("tensor"), P("tensor", None)) + (P(),) * 3
    outs += (P(None, "dp", "tensor"),)

    def step(*args):
        return local(*args, n_dp=mesh.shape["dp"], n_tensor=mesh.shape["tensor"])

    return jax.shard_map(step, mesh=mesh, in_specs=ins, out_specs=outs, check_vma=False)
```
